128 devices in a mesh: tm: 16 (over z, x), pack: 8 (over y, core).
Axes of the slice: x: 4, y: 4, z: 4, core: 2. Of those that a mesh axis runs over, the one named last changes fastest.
Arguments:
- queries: bfloat16 [8, 8192, 1024], P('pack', 'tm'), may hold values from -8 to 8
- keys: bfloat16 [8, 8192, 1024], P('pack', 'tm'), may hold values from -8 to 8
- values: bfloat16 [8, 8192, 1024], P('pack', 'tm'), may hold values from -6 to 6
- w_out: bfloat16 [1024, 1024], replicated, may hold values from -0.1875 to 0.1875
- norm_gain: float32 [1024], replicated, may hold values from 0.1 to 1.9
- block_owner: int32 [8, 64, 1], P('pack', 'tm'), may hold values from 0 to 7; in each aligned block of 4 rows (0 to 3, 4 to 7, ..., all dimensions but the last counted through in order) at most 2 rows name the same one
- block_base: int32 [8, 64], P('pack', 'tm'), may hold values from 0 to 112
- frame_offset: int32 [8, 64, 128], P('pack', 'tm'), may hold values from 0 to 15, never falling along the last dimension, each value on 1 to 16 neighbouring positions
Outputs:
- encoded: bfloat16 [8, 8192, 1024], P('pack', 'tm')
- pooled: bfloat16 [8, 2048, 1024], P('pack', 'tm')
The draws below stay inside these ranges and needn't reach their ends.
Inputs may be any that keep to these rules, and one draw needn't show every extreme that they name: `block_owner`: among the 4 blocks of one device (aligned runs of the list), at most 2 name the same owner. `frame_offset`: within each block of 128 frames the offsets never fall and each of 0 to 15 occurs.
All inputs are finite; a program needn't handle non-finite values.
Results may differ from the reference program's by a relative error of at most 0.008.
Values may be sent and summed in bfloat16 or wider, within the bound.
A program may use at most 128 MiB of HBM per device.

```python
import math
import jax
import jax.numpy as jnp
import numpy as np
from jax import lax

D = 1024
HEADS = 16
LANDMARKS = 256
TOK_DEV = 512
BLOCK = 128
WINDOW = 16
POOL_DEV = 128
GROUPS = 8
GROUP_FRAMES = 8192
ALL_LAND = 4096
DEV_BLOCKS = 4
GROUP_BLOCKS = 64
CAPACITY = 2
N_TM = 16


def drawn_field(key, own_salt):
    background = jnp.clip(jax.random.normal(jax.random.fold_in(key, own_salt), (GROUPS, N_TM, TOK_DEV, D), jnp.float32), -6.0, 6.0)
    aligned = background
    return aligned.reshape(GROUPS, GROUP_FRAMES, D)


def draw_queries(key, part):
    return drawn_field(key, 11).astype(jnp.bfloat16)


def draw_keys(key, part):
    return drawn_field(key, 12).astype(jnp.bfloat16)


def set_ends(values, key, least, largest):
    spot = [jax.random.randint(jax.random.fold_in(key, axis), (), 0, length) for axis, length in enumerate(values.shape)]
    widest = values.shape.index(max(values.shape))
    beside = spot[:widest] + [(spot[widest] + 1) % values.shape[widest]] + spot[widest + 1:]
    return values.at[tuple(spot)].set(least).at[tuple(beside)].set(largest)


def block_scale(rng, extent, cuts, smallest, largest):
    factor_of, own = 1.0, jax.random.fold_in(rng, 6)
    for dim, shards_of in cuts:
        draws = jnp.exp(jax.random.uniform(jax.random.fold_in(own, dim), (shards_of,), jnp.float32, smallest / len(cuts), largest / len(cuts)))
        factor_of = factor_of * jnp.repeat(draws, extent[dim] // shards_of).reshape([-1 if axis == dim else 1 for axis in range(len(extent))])
    return factor_of


def split_up(number_of, total, reach, skew):
    weights = [(1 << 20) // math.isqrt(standing ** skew) + 1 for standing in range(2, number_of + 1)]
    spare, given = total - reach - (number_of - 1), [1] * (number_of - 1)
    while spare > 0:
        candidates = [i for i in range(number_of - 1) if given[i] < reach]
        whole, budget = sum([weights[i] for i in candidates]), spare
        for i in candidates:
            addition = min(reach - given[i], max(1, budget * weights[i] // whole), spare)
            given[i] = given[i] + addition
            spare = spare - addition
    return np.array([reach] + given)


def ragged_sizes(rng, number_of, total, most, slope):
    if number_of == 2:
        one = jax.random.randint(rng, (), max(1, total - most), min(most, total - 1) + 1)
        return jnp.stack([one, total - one])
    tallies = jnp.asarray(split_up(number_of, total, most, slope), jnp.int32)
    twos = (number_of - 1) // 2
    giver, sink = tallies[1:1 + 2 * twos:2], tallies[2:2 + 2 * twos:2]
    slack = jnp.minimum(giver - 1, most - sink)
    passed = jax.random.randint(jax.random.fold_in(rng, 1), (twos,), 0, 1 << 20) % (slack + 1)
    tallies = tallies.at[1:1 + 2 * twos:2].set(giver - passed).at[2:2 + 2 * twos:2].set(sink + passed)
    return tallies[jax.random.permutation(jax.random.fold_in(rng, 2), number_of)]


def routed_block(stream_key, own, number, rows, amount, top, limit, slope):
    order = jax.random.permutation(stream_key, amount)
    packed, ordinary = portions_of(amount, rows * top, limit, slope, True), portions_of(amount, rows * top, limit, slope, False)
    places = jnp.arange(amount)

    def named(lengths, turn):
        used = int((lengths > 0).sum())
        fixed = max(1, used // 4)
        shifted = fixed + (places - fixed + turn * (used - fixed)) % max(1, amount - fixed)
        return jnp.zeros((amount,), jnp.int32).at[order[jnp.where(places < fixed, places, shifted)]].set(jnp.asarray(lengths, jnp.int32))

    lengths = jnp.where(number % 4 == 0, named(packed, number // 4), named(ordinary, number - number // 4 - 1))
    mixed = jax.random.permutation(jax.random.fold_in(own, 3), amount)
    giver, taker = mixed[0:amount // 2 * 2:2], mixed[1:amount // 2 * 2:2]
    margin = jnp.minimum(lengths[giver] - 1, limit - lengths[taker]) // 2
    margin = jnp.where((giver == order[0]) | (taker == order[0]) | (lengths[taker] == 0), 0, jnp.maximum(margin, 0))
    shifted = jax.random.randint(jax.random.fold_in(own, 4), (amount // 2,), 0, 1 << 20) % (margin + 1)
    lengths = lengths.at[giver].add(-shifted).at[taker].add(shifted)
    items = jnp.searchsorted(jnp.cumsum(lengths), jnp.arange(rows * top), side="right").astype(jnp.int32)
    grid = items.reshape(top, rows).T
    grid = grid[jax.random.permutation(jax.random.fold_in(own, 1), rows)]
    turn = jax.random.randint(jax.random.fold_in(own, 2), (rows, 1), 0, top)
    return jnp.take_along_axis(grid, (jnp.arange(top)[None, :] + turn) % top, axis=1)


def portions_of(number_of, total, limit, slope, full):
    weights = [(1 << 20) // math.isqrt(rank ** slope) + 1 for rank in range(1, number_of + 1)]
    largest = limit if full else min(limit, max(-(-total // number_of), total * weights[0] // sum(weights)))
    least = 1 if total - largest >= number_of - 1 else 0
    holding, rest = [largest] + [least] * (number_of - 1), total - largest - least * (number_of - 1)
    while rest > 0:
        free = [i for i in range(1, number_of) if holding[i] < largest] or [i for i in range(1, number_of) if holding[i] < limit]
        pool, budget = sum([weights[i] for i in free]), rest
        for i in free:
            extra = min(limit - holding[i], max(1, budget * weights[i] // pool), rest)
            holding[i] = holding[i] + extra
            rest = rest - extra
    return np.array(holding)


def scatter_about(own_key, shape, scale, limit, shards=(), held_as=jnp.bfloat16):
    gain = block_scale(own_key, shape, shards, -0.22, 0.18) if shards else 1.0
    drawn = jax.random.normal(own_key, shape, jnp.float32) * scale * gain
    return jnp.minimum(jnp.maximum(drawn, -limit), limit).astype(held_as)


def setup_inputs(seed: int = 0) -> dict:
    seeds = jax.random.split(jax.random.key(seed), 9)
    queries = draw_queries(jax.random.fold_in(seeds[8], 71), 0)
    keys = draw_keys(jax.random.fold_in(seeds[8], 71), 0)
    values = scatter_about(seeds[2], (GROUPS, GROUP_FRAMES, D), 1.0, 6.0, ((0, 8), (1, 16)))
    w_out = scatter_about(seeds[3], (D, D), D ** -0.5, 0.1875)
    norm_gain = jnp.clip(1.0 + 0.18 * jax.random.normal(seeds[4], (D,), jnp.float32), 0.1, 1.9)
    block_owner_keys = jax.random.split(jax.random.fold_in(seeds[5], 1), GROUPS * GROUP_BLOCKS // DEV_BLOCKS)
    block_owner_turns = jax.random.permutation(jax.random.fold_in(seeds[5], 3), GROUPS * GROUP_BLOCKS // DEV_BLOCKS)
    block_owner = jax.vmap(lambda own, number: routed_block(jax.random.fold_in(seeds[5], 2), own, number, DEV_BLOCKS, GROUPS, 1, CAPACITY, 2))(block_owner_keys, block_owner_turns).reshape((GROUPS, GROUP_BLOCKS, 1))
    block_base = set_ends(jax.random.randint(seeds[6], (GROUPS, GROUP_BLOCKS), 0, POOL_DEV - WINDOW + 1), jax.random.fold_in(seeds[6], 1), 0, POOL_DEV - WINDOW).astype(jnp.int32)
    frame_offset = jax.vmap(lambda own: jnp.searchsorted(jnp.cumsum(ragged_sizes(own, WINDOW, BLOCK, WINDOW, 1)), jnp.arange(BLOCK), side="right"))(jax.random.split(seeds[7], GROUPS * GROUP_BLOCKS)).reshape((GROUPS, GROUP_BLOCKS, BLOCK)).astype(jnp.int32)
    return {"queries": queries, "keys": keys, "values": values, "w_out": w_out, "norm_gain": norm_gain, "block_owner": block_owner, "block_base": block_base, "frame_offset": frame_offset}


def landmark_means(frames):
    span = TOK_DEV // LANDMARKS
    summed = frames.astype(jnp.float32).reshape(-1, span, D)
    return lax.optimization_barrier(jnp.mean(summed, axis=1)).astype(jnp.bfloat16)

def attend(query_rows, key_rows, value_rows):
    row_count = query_rows.shape[0]
    head_dim = D // HEADS
    query_heads = query_rows.astype(jnp.float32).reshape(row_count, HEADS, head_dim)
    key_heads = key_rows.astype(jnp.float32).reshape(-1, HEADS, head_dim)
    value_heads = value_rows.astype(jnp.float32).reshape(-1, HEADS, head_dim)
    scores = jnp.einsum('nhe,mhe->nhm', query_heads, key_heads) * head_dim ** (-0.5)
    weights = jnp.exp(scores - lax.optimization_barrier(jnp.max(scores, axis=-1, keepdims=True)))
    totals = lax.optimization_barrier(jnp.sum(weights, axis=-1))
    rounded = lax.optimization_barrier(weights.astype(jnp.bfloat16)).astype(jnp.float32)
    blended = jnp.einsum('nhm,mhe->nhe', rounded, value_heads) / totals[..., None]
    return blended.reshape(row_count, D).astype(jnp.bfloat16)

def reference(queries, keys, values, w_out, norm_gain, block_owner, block_base, frame_offset):
    row_block = math.gcd(GROUP_FRAMES, 512)
    encoded_groups = []
    for group_index in range(GROUPS):
        group_q = queries[group_index]
        group_k = keys[group_index]
        group_v = values[group_index]
        mark_q = landmark_means(group_q)
        mark_k = landmark_means(group_k)
        mark_v = lax.map(lambda pieces: attend(pieces[0], pieces[1], pieces[2]), (mark_q.reshape(N_TM, LANDMARKS, D), group_k.reshape(N_TM, TOK_DEV, D), group_v.reshape(N_TM, TOK_DEV, D))).reshape(ALL_LAND, D)
        attended = lax.map(lambda frame_block: attend(frame_block, mark_k, mark_v), group_q.reshape(-1, row_block, D)).reshape(GROUP_FRAMES, D)
        projected = jnp.dot(attended, w_out, preferred_element_type=jnp.float32)
        scaled = projected * lax.rsqrt(lax.optimization_barrier(jnp.mean(projected * projected, axis=-1, keepdims=True)) + 1e-06)
        encoded_groups.append((scaled * norm_gain).astype(jnp.bfloat16))
    encoded = jnp.stack(encoded_groups)
    positions = jnp.arange(GROUP_FRAMES, dtype=jnp.int32)
    shard_of = positions // TOK_DEV
    owner_of = jnp.repeat(block_owner[:, :, 0], BLOCK, axis=1)
    base_of = jnp.repeat(block_base, BLOCK, axis=1)
    target = (owner_of * N_TM + shard_of[None, :]) * POOL_DEV + base_of + frame_offset.reshape(GROUPS, GROUP_FRAMES)
    flat_target = target.reshape(-1).astype(jnp.int32)
    segment_total = GROUPS * N_TM * POOL_DEV
    pool_sums = jax.ops.segment_sum(encoded.reshape(-1, D).astype(jnp.float32), flat_target, num_segments=segment_total)
    counts = jax.ops.segment_sum(jnp.ones(flat_target.shape, jnp.float32), flat_target, num_segments=segment_total)
    pooled = (pool_sums / jnp.maximum(counts, 1.0)[:, None]).astype(jnp.bfloat16).reshape(GROUPS, N_TM * POOL_DEV, D)
    return (encoded, pooled)
```

```python
import functools

import jax
import jax.numpy as jnp
from jax import lax
from jax.experimental import pallas as pl
from jax.experimental.pallas import tpu as pltpu
from jax.sharding import PartitionSpec as P

HEAD = 64
LANE = 128
LANDMARKS = 256
BLOCK = 128
WINDOW = 16
CAPACITY = 2
POOL_DEV = 128
F32 = jnp.float32
BF16 = jnp.bfloat16
I32 = jnp.int32
MESH = pl.DeviceIdType.MESH
EXP_SCALE = HEAD**-0.5 * 1.4426950408889634


def dot_t(a, b):
    return lax.dot_general(a, b, (((1,), (1,)), ((), ())), preferred_element_type=F32)


def dot(a, b):
    return jnp.dot(a, b, preferred_element_type=F32)


def swap_halves(x):
    return pltpu.roll(x, HEAD, 1)


def body(
    n_tm,
    n_pack,
    chunk,
    q_hbm,
    k_hbm,
    v_hbm,
    w_hbm,
    gain_ref,
    owner_ref,
    base_ref,
    offset_ref,
    enc_hbm,
    pooled_ref,
    q_v,
    k_v,
    v_v,
    w_v,
    mark_q,
    q_out,
    q_in,
    kv_out,
    kv_in,
    k_wide,
    v_wide,
    s_a,
    s_b,
    top_a,
    top_b,
    o_out,
    o_in,
    attended,
    enc_v,
    one_hot,
    tags_out,
    tags_in,
    pool_out,
    pool_in,
    load_sem,
    q_send,
    q_recv,
    kv_send,
    kv_recv,
    o_send,
    o_recv,
    tag_send,
    tag_recv,
    pool_send,
    pool_recv,
    store_sem,
):
    me = lax.axis_index("tm")
    pk = lax.axis_index("pack")
    frames, width = q_v.shape
    half_rows = frames // 2
    lands = n_tm * LANDMARKS
    pairs = width // LANE

    loads = [
        pltpu.make_async_copy(src.at[0] if i < 3 else src, dst, load_sem.at[i])
        for i, (src, dst) in enumerate(((q_hbm, q_v), (k_hbm, k_v), (v_hbm, v_v), (w_hbm, w_v)))
    ]
    for load in loads:
        load.start()

    barrier = pltpu.get_barrier_semaphore()

    def greet_tm(r, c):
        pl.semaphore_signal(
            barrier, inc=1, device_id={"tm": lax.rem(me + r, n_tm)}, device_id_type=MESH
        )
        return c

    def greet_pack(r, c):
        pl.semaphore_signal(
            barrier, inc=1, device_id={"pack": lax.rem(pk + r, n_pack)}, device_id_type=MESH
        )
        return c

    lax.fori_loop(1, n_tm, greet_tm, 0)
    lax.fori_loop(1, n_pack, greet_pack, 0)

    def tm_copy(src, dst, send, recv, peer, source):
        return pltpu.make_async_remote_copy(
            src_ref=src.at[peer],
            dst_ref=dst.at[source],
            send_sem=send.at[peer],
            recv_sem=recv.at[source],
            device_id={"tm": peer},
            device_id_type=MESH,
        )

    def pack_copy(src, dst, send, recv, peer, source):
        return pltpu.make_async_remote_copy(
            src_ref=src.at[peer],
            dst_ref=dst.at[source],
            send_sem=send.at[peer],
            recv_sem=recv.at[source],
            device_id={"pack": peer},
            device_id_type=MESH,
        )

    lane = lax.broadcasted_iota(I32, (half_rows, LANE), 1)
    low = lane < HEAD

    slot_rows = CAPACITY * WINDOW
    out_rows = n_pack * slot_rows
    n_blocks = offset_ref.shape[0]
    row_id = lax.broadcasted_iota(I32, (out_rows, LANE), 0)
    owner_id = row_id // slot_rows
    slot_id = (row_id // WINDOW) % CAPACITY
    window_id = row_id % WINDOW
    target = jnp.full((out_rows, LANE), -1, I32)
    tally = jnp.zeros((out_rows, LANE), F32)
    for b in range(n_blocks):
        owner = owner_ref[0, b]
        rank = jnp.int32(0)
        for earlier in range(b):
            rank = rank + jnp.where(owner_ref[0, earlier] == owner, 1, 0)
        mine = (owner_id == owner) & (slot_id == rank)
        target = jnp.where(mine, window_id + base_ref[0, b], target)
        hit = mine & (window_id == offset_ref[b : b + 1, :])
        hit = jnp.where(hit, 1.0, 0.0)
        tally = tally + jnp.sum(hit, axis=1, keepdims=True)
        one_hot[:, b * BLOCK : (b + 1) * BLOCK] = hit.astype(BF16)
    tag_lane = lax.broadcasted_iota(I32, (out_rows, LANE), 1)
    tags = jnp.where(tag_lane == 0, target.astype(F32), tally).astype(BF16)
    for o in range(n_pack):
        tags_out[o] = tags[o * slot_rows : (o + 1) * slot_rows, :]

    average = jnp.where(
        lax.broadcasted_iota(I32, (LANDMARKS, frames), 1) // 2
        == lax.broadcasted_iota(I32, (LANDMARKS, frames), 0),
        0.5,
        0.0,
    ).astype(BF16)

    loads[0].wait()

    def pack_queries(j, c):
        cols = pl.ds(pl.multiple_of(j * LANE, LANE), LANE)
        upper = q_v[0:half_rows, cols].astype(F32)
        lower = q_v[half_rows:frames, cols].astype(F32)
        q_out[2 * j] = jnp.where(low, upper, swap_halves(lower)).astype(BF16)
        q_out[2 * j + 1] = jnp.where(low, swap_halves(upper), lower).astype(BF16)
        mark_q[:, cols] = dot(average, q_v[:, cols]).astype(BF16)
        return c

    lax.fori_loop(0, pairs, pack_queries, 0)

    pl.semaphore_wait(barrier, n_tm + n_pack - 2)

    def send_queries(r, c):
        tm_copy(q_out, q_in, q_send, q_recv, lax.rem(me + r, n_tm), me).start()
        return c

    lax.fori_loop(1, n_tm, send_queries, 0)
    q_in[me] = q_out[me]

    def send_tags(r, c):
        pack_copy(tags_out, tags_in, tag_send, tag_recv, lax.rem(pk + r, n_pack), pk).start()
        return c

    lax.fori_loop(1, n_pack, send_tags, 0)
    tags_in[pk] = tags_out[pk]

    loads[1].wait()
    loads[2].wait()

    def summarize(step, c):
        j = lax.rem(me // 2 + step, pairs)
        cols = pl.ds(pl.multiple_of(j * LANE, LANE), LANE)
        keys = k_v[:, cols]
        mk = dot(average, keys).astype(BF16).astype(F32)
        mq = mark_q[:, cols].astype(F32)
        vals = v_v[:, cols]
        parts = []
        for head in range(2):
            chosen = low if head == 0 else ~low
            s = dot_t(jnp.where(chosen, mq, 0.0).astype(BF16), keys)
            p = jnp.exp2((s - jnp.max(s, axis=1, keepdims=True)) * EXP_SCALE)
            total = jnp.sum(p, axis=1, keepdims=True)
            parts.append(dot(p.astype(BF16), vals) / total)
        mv = jnp.where(low, parts[0], parts[1])
        kv_out[2 * j] = jnp.where(low, mk, swap_halves(mv)).astype(BF16)
        kv_out[2 * j + 1] = jnp.where(low, swap_halves(mk), mv).astype(BF16)
        for head in range(2):
            peer = 2 * j + head

            @pl.when(peer != me)
            def _():
                tm_copy(kv_out, kv_in, kv_send, kv_recv, peer, me).start()

            @pl.when(peer == me)
            def _():
                kv_in[me] = kv_out[me]

        return c

    lax.fori_loop(0, pairs, summarize, 0)

    def widen(i, c):
        source = lax.rem(me + n_tm - i, n_tm)

        @pl.when(source != me)
        def _():
            tm_copy(kv_out, kv_in, kv_send, kv_recv, source, source).wait_recv()

        rows = pl.ds(pl.multiple_of(source * LANDMARKS, LANDMARKS), LANDMARKS)
        straight = kv_in[source].astype(F32)
        swapped = swap_halves(straight)
        low_land = lax.broadcasted_iota(I32, (LANDMARKS, LANE), 1) < HEAD
        k_wide[0, rows, :] = jnp.where(low_land, straight, 0.0).astype(BF16)
        k_wide[1, rows, :] = jnp.where(low_land, 0.0, swapped).astype(BF16)
        v_wide[0, rows, :] = jnp.where(low_land, swapped, 1.0).astype(BF16)
        v_wide[1, rows, :] = jnp.where(low_land, 1.0, straight).astype(BF16)
        return c

    lax.fori_loop(0, n_tm, widen, 0)

    pieces = [slice(at, at + chunk) for at in range(0, lands, chunk)]

    def score_piece(q, half, piece, s_ref, top):
        s = dot_t(q, k_wide[half, piece, :])
        s_ref[:, piece] = s
        for at in range(0, chunk, LANE):
            part = s[:, at : at + LANE]
            top = part if top is None else jnp.maximum(top, part)
        return top

    def blend_piece(half, piece, s_ref, top, acc):
        p = jnp.exp2((s_ref[:, piece] - top) * EXP_SCALE).astype(BF16)
        d = dot(p, v_wide[half, piece, :])
        return d if acc is None else acc + d

    def stage(q, half_next, s_next, top_next, half, s_now, top_now):
        top = jnp.max(top_now[...], axis=1, keepdims=True)
        following, acc = None, None
        for piece in pieces:
            if q is not None:
                following = score_piece(q, half_next, piece, s_next, following)
            acc = blend_piece(half, piece, s_now, top, acc)
        if q is not None:
            top_next[...] = following
        return acc

    def finish(source, first, second):
        o = jnp.where(low, first / first[:, HEAD : HEAD + 1], second / second[:, 0:1])
        o_out[source] = o.astype(BF16)

    following = None
    for piece in pieces:
        following = score_piece(q_in[me], 0, piece, s_a, following)
    top_a[...] = following

    def attend(i, c):
        source = lax.rem(me + n_tm - i, n_tm)
        coming = lax.rem(me + n_tm - 1 - i, n_tm)
        tm_copy(q_out, q_in, q_send, q_recv, coming, coming).wait_recv()
        first = stage(q_in[source], 1, s_b, top_b, 0, s_a, top_a)
        second = stage(q_in[coming], 0, s_a, top_a, 1, s_b, top_b)
        finish(source, first, second)

        @pl.when(i > 0)
        def _():
            tm_copy(o_out, o_in, o_send, o_recv, source, me).start()

        return c

    lax.fori_loop(0, n_tm - 1, attend, 0)
    last = lax.rem(me + 1, n_tm)
    first = stage(q_in[last], 1, s_b, top_b, 0, s_a, top_a)
    second = stage(None, None, None, None, 1, s_b, top_b)
    finish(last, first, second)
    tm_copy(o_out, o_in, o_send, o_recv, last, me).start()
    o_in[me] = o_out[me]

    def await_heads(i, c):
        source = lax.rem(me + i, n_tm)
        tm_copy(o_out, o_in, o_send, o_recv, source, source).wait_recv()
        return c

    lax.fori_loop(1, n_tm, await_heads, 0)

    def unpack(j, c):
        cols = pl.ds(pl.multiple_of(j * LANE, LANE), LANE)
        even = o_in[2 * j].astype(F32)
        odd = o_in[2 * j + 1].astype(F32)
        attended[0:half_rows, cols] = jnp.where(low, even, swap_halves(odd)).astype(BF16)
        attended[half_rows:frames, cols] = jnp.where(low, swap_halves(even), odd).astype(BF16)
        return c

    lax.fori_loop(0, pairs, unpack, 0)
    loads[3].wait()
    gain = gain_ref[...]

    def project(i, c):
        rows = pl.ds(pl.multiple_of(i * BLOCK, BLOCK), BLOCK)
        projected = dot(attended[rows, :], w_v[...])
        power = jnp.mean(projected * projected, axis=1, keepdims=True)
        enc_v[rows, :] = (projected * lax.rsqrt(power + 1e-6) * gain).astype(BF16)
        return c

    lax.fori_loop(0, frames // BLOCK, project, 0)
    store = pltpu.make_async_copy(enc_v, enc_hbm.at[0], store_sem)
    store.start()

    summed = dot(one_hot[...], enc_v[...]).astype(BF16)
    for o in range(n_pack):
        pool_out[o] = summed[o * slot_rows : (o + 1) * slot_rows, :]

    def send_pool(r, c):
        pack_copy(pool_out, pool_in, pool_send, pool_recv, lax.rem(pk + r, n_pack), pk).start()
        return c

    lax.fori_loop(1, n_pack, send_pool, 0)
    pool_in[pk] = pool_out[pk]

    def await_pool(i, c):
        source = lax.rem(pk + i, n_pack)
        pack_copy(tags_out, tags_in, tag_send, tag_recv, source, source).wait_recv()
        pack_copy(pool_out, pool_in, pool_send, pool_recv, source, source).wait_recv()
        return c

    lax.fori_loop(1, n_pack, await_pool, 0)
    tags = tags_in[...].reshape(out_rows, LANE)
    rows = tags.astype(F32)[:, 0:1].astype(I32)
    placing = jnp.where(
        rows == lax.broadcasted_iota(I32, (out_rows, POOL_DEV), 1), 1.0, 0.0
    ).astype(BF16)
    contract = (((0,), (0,)), ((), ()))
    sums = lax.dot_general(
        placing, pool_in[...].reshape(out_rows, width), contract, preferred_element_type=F32
    )
    counts = lax.dot_general(placing, tags, contract, preferred_element_type=F32)[:, 1:2]
    pooled_ref[0] = (sums / jnp.maximum(counts, 1.0)).astype(BF16)

    def drain_tm(r, c):
        peer = lax.rem(me + r, n_tm)
        tm_copy(q_out, q_in, q_send, q_recv, peer, me).wait_send()
        tm_copy(kv_out, kv_in, kv_send, kv_recv, peer, me).wait_send()
        tm_copy(o_out, o_in, o_send, o_recv, peer, me).wait_send()
        return c

    def drain_pack(r, c):
        peer = lax.rem(pk + r, n_pack)
        pack_copy(tags_out, tags_in, tag_send, tag_recv, peer, pk).wait_send()
        pack_copy(pool_out, pool_in, pool_send, pool_recv, peer, pk).wait_send()
        return c

    lax.fori_loop(1, n_tm, drain_tm, 0)
    lax.fori_loop(1, n_pack, drain_pack, 0)
    store.wait()


def local(queries, keys, values, w_out, norm_gain, block_owner, block_base, frame_offset):
    n_tm = lax.axis_size("tm")
    n_pack = lax.axis_size("pack")
    _, frames, width = queries.shape
    lands = n_tm * LANDMARKS
    half = frames // 2
    slot_rows = CAPACITY * WINDOW
    any_ref = pl.BlockSpec(memory_space=pl.ANY)
    vmem = pl.BlockSpec(memory_space=pltpu.VMEM)
    smem = pl.BlockSpec(memory_space=pltpu.SMEM)
    dma = pltpu.SemaphoreType.DMA
    call = pl.pallas_call(
        functools.partial(body, n_tm, n_pack, min(1024, lands)),
        name="landmark_layer",
        out_shape=(
            jax.ShapeDtypeStruct((1, frames, width), BF16),
            jax.ShapeDtypeStruct((1, POOL_DEV, width), BF16),
        ),
        in_specs=[any_ref] * 4 + [vmem, smem, smem, vmem],
        out_specs=(any_ref, vmem),
        scratch_shapes=[
            pltpu.VMEM((frames, width), BF16),
            pltpu.VMEM((frames, width), BF16),
            pltpu.VMEM((frames, width), BF16),
            pltpu.VMEM((width, width), BF16),
            pltpu.VMEM((LANDMARKS, width), BF16),
            pltpu.VMEM((n_tm, half, LANE), BF16),
            pltpu.VMEM((n_tm, half, LANE), BF16),
            pltpu.VMEM((n_tm, LANDMARKS, LANE), BF16),
            pltpu.VMEM((n_tm, LANDMARKS, LANE), BF16),
            pltpu.VMEM((2, lands, LANE), BF16),
            pltpu.VMEM((2, lands, LANE), BF16),
            pltpu.VMEM((half, lands), F32),
            pltpu.VMEM((half, lands), F32),
            pltpu.VMEM((half, LANE), F32),
            pltpu.VMEM((half, LANE), F32),
            pltpu.VMEM((n_tm, half, LANE), BF16),
            pltpu.VMEM((n_tm, half, LANE), BF16),
            pltpu.VMEM((frames, width), BF16),
            pltpu.VMEM((frames, width), BF16),
            pltpu.VMEM((n_pack * slot_rows, frames), BF16),
            pltpu.VMEM((n_pack, slot_rows, LANE), BF16),
            pltpu.VMEM((n_pack, slot_rows, LANE), BF16),
            pltpu.VMEM((n_pack, slot_rows, width), BF16),
            pltpu.VMEM((n_pack, slot_rows, width), BF16),
            dma((4,)),
            dma((n_tm,)),
            dma((n_tm,)),
            dma((n_tm,)),
            dma((n_tm,)),
            dma((n_tm,)),
            dma((n_tm,)),
            dma((n_pack,)),
            dma((n_pack,)),
            dma((n_pack,)),
            dma((n_pack,)),
            dma(()),
        ],
        compiler_params=pltpu.CompilerParams(
            collective_id=0, has_side_effects=True, vmem_limit_bytes=56 << 20
        ),
        cost_estimate=pl.CostEstimate(
            flops=20_000_000_000, bytes_accessed=8_000_000, transcendentals=36_000_000
        ),
    )
    return call(
        queries,
        keys,
        values,
        w_out,
        norm_gain.reshape(1, width),
        block_owner.reshape(1, -1),
        block_base,
        frame_offset[0],
    )


def solution(mesh):
    return jax.shard_map(
        local,
        mesh=mesh,
        in_specs=(
            P("pack", "tm", None),
            P("pack", "tm", None),
            P("pack", "tm", None),
            P(),
            P(),
            P("pack", "tm", None),
            P("pack", "tm"),
            P("pack", "tm", None),
        ),
        out_specs=(P("pack", "tm", None), P("pack", "tm", None)),
        check_vma=False,
    )
```

```python
import functools

import jax
import jax.numpy as jnp
from jax import lax
from jax.experimental import pallas as pl
from jax.experimental.pallas import tpu as pltpu
from jax.sharding import PartitionSpec as P

HEAD = 64
LANE = 128
LANDMARKS = 256
BLOCK = 128
WINDOW = 16
CAPACITY = 2
POOL_DEV = 128
F32 = jnp.float32
BF16 = jnp.bfloat16
I32 = jnp.int32
MESH = pl.DeviceIdType.MESH
EXP_SCALE = HEAD**-0.5 * 1.4426950408889634


def dot_t(a, b):
    return lax.dot_general(a, b, (((1,), (1,)), ((), ())), preferred_element_type=F32)


def dot(a, b):
    return jnp.dot(a, b, preferred_element_type=F32)


def swap_halves(x):
    return pltpu.roll(x, HEAD, 1)


def body(
    n_tm,
    n_pack,
    chunk,
    q_hbm,
    k_hbm,
    v_hbm,
    w_hbm,
    gain_ref,
    owner_ref,
    base_ref,
    offset_ref,
    enc_hbm,
    pooled_ref,
    q_v,
    k_v,
    v_v,
    w_v,
    q_out,
    q_in,
    k_out,
    k_in,
    v_out,
    v_in,
    k_wide,
    v_wide,
    s_a,
    s_b,
    top_a,
    top_b,
    o_out,
    o_in,
    attended,
    enc_v,
    one_hot,
    tags_out,
    tags_in,
    pool_out,
    pool_in,
    load_sem,
    q_send,
    q_recv,
    k_send,
    k_recv,
    v_send,
    v_recv,
    o_send,
    o_recv,
    tag_send,
    tag_recv,
    pool_send,
    pool_recv,
    store_sem,
):
    me = lax.axis_index("tm")
    pk = lax.axis_index("pack")
    frames, width = q_v.shape
    half_rows = frames // 2
    lands = n_tm * LANDMARKS
    pairs = width // LANE

    loads = [
        pltpu.make_async_copy(src.at[0] if i < 3 else src, dst, load_sem.at[i])
        for i, (src, dst) in enumerate(((k_hbm, k_v), (q_hbm, q_v), (v_hbm, v_v), (w_hbm, w_v)))
    ]
    for load in loads:
        load.start()

    barrier = pltpu.get_barrier_semaphore()

    def greet_tm(r, c):
        pl.semaphore_signal(
            barrier, inc=1, device_id={"tm": lax.rem(me + r, n_tm)}, device_id_type=MESH
        )
        return c

    def greet_pack(r, c):
        pl.semaphore_signal(
            barrier, inc=1, device_id={"pack": lax.rem(pk + r, n_pack)}, device_id_type=MESH
        )
        return c

    lax.fori_loop(1, n_tm, greet_tm, 0)
    lax.fori_loop(1, n_pack, greet_pack, 0)

    def tm_copy(src, dst, send, recv, peer, source):
        return pltpu.make_async_remote_copy(
            src_ref=src.at[peer],
            dst_ref=dst.at[source],
            send_sem=send.at[peer],
            recv_sem=recv.at[source],
            device_id={"tm": peer},
            device_id_type=MESH,
        )

    def pack_copy(src, dst, send, recv, peer, source):
        return pltpu.make_async_remote_copy(
            src_ref=src.at[peer],
            dst_ref=dst.at[source],
            send_sem=send.at[peer],
            recv_sem=recv.at[source],
            device_id={"pack": peer},
            device_id_type=MESH,
        )

    lane = lax.broadcasted_iota(I32, (half_rows, LANE), 1)
    low = lane < HEAD

    slot_rows = CAPACITY * WINDOW
    out_rows = n_pack * slot_rows
    n_blocks = offset_ref.shape[0]
    row_id = lax.broadcasted_iota(I32, (out_rows, LANE), 0)
    owner_id = row_id // slot_rows
    slot_id = (row_id // WINDOW) % CAPACITY
    window_id = row_id % WINDOW
    target = jnp.full((out_rows, LANE), -1, I32)
    tally = jnp.zeros((out_rows, LANE), F32)
    for b in range(n_blocks):
        owner = owner_ref[0, b]
        rank = jnp.int32(0)
        for earlier in range(b):
            rank = rank + jnp.where(owner_ref[0, earlier] == owner, 1, 0)
        mine = (owner_id == owner) & (slot_id == rank)
        target = jnp.where(mine, window_id + base_ref[0, b], target)
        hit = mine & (window_id == offset_ref[b : b + 1, :])
        hit = jnp.where(hit, 1.0, 0.0)
        tally = tally + jnp.sum(hit, axis=1, keepdims=True)
        one_hot[:, b * BLOCK : (b + 1) * BLOCK] = hit.astype(BF16)
    tag_lane = lax.broadcasted_iota(I32, (out_rows, LANE), 1)
    tags = jnp.where(tag_lane == 0, target.astype(F32), tally).astype(BF16)
    for o in range(n_pack):
        tags_out[o] = tags[o * slot_rows : (o + 1) * slot_rows, :]

    average = jnp.where(
        lax.broadcasted_iota(I32, (LANDMARKS, frames), 1) // 2
        == lax.broadcasted_iota(I32, (LANDMARKS, frames), 0),
        0.5,
        0.0,
    ).astype(BF16)

    land_rows = LANDMARKS // 2
    low_land = lax.broadcasted_iota(I32, (land_rows, LANE), 1) < HEAD

    def fold(ref, j, x, mask):
        upper, lower = x[: x.shape[0] // 2], x[x.shape[0] // 2 :]
        ref[2 * j] = jnp.where(mask, upper, swap_halves(lower)).astype(BF16)
        ref[2 * j + 1] = jnp.where(mask, swap_halves(upper), lower).astype(BF16)

    def pair_columns(j):
        return pl.ds(pl.multiple_of(j * LANE, LANE), LANE)

    loads[0].wait()

    def mark_keys(j, c):
        means = dot(average, k_v[:, pair_columns(j)])
        fold(k_out, j, means.astype(BF16).astype(F32), low_land)
        return c

    lax.fori_loop(0, pairs, mark_keys, 0)
    loads[1].wait()

    def pack_queries(j, c):
        fold(q_out, j, q_v[:, pair_columns(j)].astype(F32), low)
        return c

    lax.fori_loop(0, pairs, pack_queries, 0)

    pl.semaphore_wait(barrier, n_tm + n_pack - 2)

    def send_keys(r, c):
        tm_copy(k_out, k_in, k_send, k_recv, lax.rem(me + r, n_tm), me).start()
        return c

    lax.fori_loop(1, n_tm, send_keys, 0)
    k_in[me] = k_out[me]

    loads[2].wait()

    def summarize(step, c):
        j = lax.rem(me // 2 + step, pairs)
        cols = pair_columns(j)
        keys, vals = k_v[:, cols], v_v[:, cols]
        mq = dot(average, q_v[:, cols])
        parts = []
        for head in range(2):
            chosen = low if head == 0 else ~low
            s = dot_t(jnp.where(chosen, mq, 0.0).astype(BF16), keys)
            p = jnp.exp2((s - jnp.max(s, axis=1, keepdims=True)) * EXP_SCALE)
            total = jnp.sum(p, axis=1, keepdims=True)
            parts.append(dot(p.astype(BF16), vals) / total)
        fold(v_out, j, jnp.where(low, parts[0], parts[1]), low_land)
        for head in range(2):
            peer = 2 * j + head

            @pl.when(peer != me)
            def _():
                tm_copy(v_out, v_in, v_send, v_recv, peer, me).start()

        return c

    lax.fori_loop(0, pairs, summarize, 0)
    v_in[me] = v_out[me]

    def send_queries(r, c):
        tm_copy(q_out, q_in, q_send, q_recv, lax.rem(me + r, n_tm), me).start()
        return c

    lax.fori_loop(1, n_tm, send_queries, 0)
    q_in[me] = q_out[me]

    def send_tags(r, c):
        pack_copy(tags_out, tags_in, tag_send, tag_recv, lax.rem(pk + r, n_pack), pk).start()
        return c

    lax.fori_loop(1, n_pack, send_tags, 0)
    tags_in[pk] = tags_out[pk]

    def widen(arrived, send, recv, out, wide, filler):
        def one(i, c):
            source = lax.rem(me + n_tm - i, n_tm)

            @pl.when(source != me)
            def _():
                tm_copy(out, arrived, send, recv, source, source).wait_recv()

            at = pl.multiple_of(source * LANDMARKS, LANDMARKS)
            upper = pl.ds(at, land_rows)
            lower = pl.ds(at + land_rows, land_rows)
            straight = arrived[source].astype(F32)
            swapped = swap_halves(straight)
            wide[0, upper, :] = jnp.where(low_land, straight, filler).astype(BF16)
            wide[0, lower, :] = jnp.where(low_land, swapped, filler).astype(BF16)
            wide[1, upper, :] = jnp.where(low_land, filler, swapped).astype(BF16)
            wide[1, lower, :] = jnp.where(low_land, filler, straight).astype(BF16)
            return c

        lax.fori_loop(0, n_tm, one, 0)

    widen(k_in, k_send, k_recv, k_out, k_wide, 0.0)

    pieces = [slice(at, at + chunk) for at in range(0, lands, chunk)]

    def score_piece(q, half, piece, s_ref, top):
        s = dot_t(q, k_wide[half, piece, :])
        s_ref[:, piece] = s
        for at in range(0, chunk, LANE):
            part = s[:, at : at + LANE]
            top = part if top is None else jnp.maximum(top, part)
        return top

    def blend_piece(half, piece, s_ref, top, acc):
        p = jnp.exp2((s_ref[:, piece] - top) * EXP_SCALE).astype(BF16)
        d = dot(p, v_wide[half, piece, :])
        return d if acc is None else acc + d

    def stage(q, half_next, s_next, top_next, half, s_now, top_now):
        top = jnp.max(top_now[...], axis=1, keepdims=True)
        following, acc = None, None
        for piece in pieces:
            if q is not None:
                following = score_piece(q, half_next, piece, s_next, following)
            acc = blend_piece(half, piece, s_now, top, acc)
        if q is not None:
            top_next[...] = following
        return acc

    def finish(source, first, second):
        o = jnp.where(low, first / first[:, HEAD : HEAD + 1], second / second[:, 0:1])
        o_out[source] = o.astype(BF16)

    following = None
    for piece in pieces:
        following = score_piece(q_in[me], 0, piece, s_a, following)
    top_a[...] = following
    widen(v_in, v_send, v_recv, v_out, v_wide, 1.0)

    def attend(i, c):
        source = lax.rem(me + n_tm - i, n_tm)
        coming = lax.rem(me + n_tm - 1 - i, n_tm)
        tm_copy(q_out, q_in, q_send, q_recv, coming, coming).wait_recv()
        first = stage(q_in[source], 1, s_b, top_b, 0, s_a, top_a)
        second = stage(q_in[coming], 0, s_a, top_a, 1, s_b, top_b)
        finish(source, first, second)

        @pl.when(i > 0)
        def _():
            tm_copy(o_out, o_in, o_send, o_recv, source, me).start()

        return c

    lax.fori_loop(0, n_tm - 1, attend, 0)
    last = lax.rem(me + 1, n_tm)
    first = stage(q_in[last], 1, s_b, top_b, 0, s_a, top_a)
    second = stage(None, None, None, None, 1, s_b, top_b)
    finish(last, first, second)
    tm_copy(o_out, o_in, o_send, o_recv, last, me).start()
    o_in[me] = o_out[me]

    def await_heads(i, c):
        source = lax.rem(me + i, n_tm)
        tm_copy(o_out, o_in, o_send, o_recv, source, source).wait_recv()
        return c

    lax.fori_loop(1, n_tm, await_heads, 0)

    def unpack(j, c):
        cols = pl.ds(pl.multiple_of(j * LANE, LANE), LANE)
        even = o_in[2 * j].astype(F32)
        odd = o_in[2 * j + 1].astype(F32)
        attended[0:half_rows, cols] = jnp.where(low, even, swap_halves(odd)).astype(BF16)
        attended[half_rows:frames, cols] = jnp.where(low, swap_halves(even), odd).astype(BF16)
        return c

    lax.fori_loop(0, pairs, unpack, 0)
    loads[3].wait()
    gain = gain_ref[...]

    def project(i, c):
        rows = pl.ds(pl.multiple_of(i * half_rows, half_rows), half_rows)
        projected = dot(attended[rows, :], w_v[...])
        power = jnp.mean(projected * projected, axis=1, keepdims=True)
        enc_v[rows, :] = (projected * lax.rsqrt(power + 1e-6) * gain).astype(BF16)
        return c

    lax.fori_loop(0, 2, project, 0)
    store = pltpu.make_async_copy(enc_v, enc_hbm.at[0], store_sem)
    store.start()

    summed = dot(one_hot[...], enc_v[...]).astype(BF16)
    for o in range(n_pack):
        pool_out[o] = summed[o * slot_rows : (o + 1) * slot_rows, :]

    def send_pool(r, c):
        pack_copy(pool_out, pool_in, pool_send, pool_recv, lax.rem(pk + r, n_pack), pk).start()
        return c

    lax.fori_loop(1, n_pack, send_pool, 0)
    pool_in[pk] = pool_out[pk]

    def await_pool(i, c):
        source = lax.rem(pk + i, n_pack)
        pack_copy(tags_out, tags_in, tag_send, tag_recv, source, source).wait_recv()
        pack_copy(pool_out, pool_in, pool_send, pool_recv, source, source).wait_recv()
        return c

    lax.fori_loop(1, n_pack, await_pool, 0)
    tags = tags_in[...].reshape(out_rows, LANE)
    rows = tags.astype(F32)[:, 0:1].astype(I32)
    placing = jnp.where(
        rows == lax.broadcasted_iota(I32, (out_rows, POOL_DEV), 1), 1.0, 0.0
    ).astype(BF16)
    contract = (((0,), (0,)), ((), ()))
    sums = lax.dot_general(
        placing, pool_in[...].reshape(out_rows, width), contract, preferred_element_type=F32
    )
    counts = lax.dot_general(placing, tags, contract, preferred_element_type=F32)[:, 1:2]
    pooled_ref[0] = (sums / jnp.maximum(counts, 1.0)).astype(BF16)

    def drain_tm(r, c):
        peer = lax.rem(me + r, n_tm)
        tm_copy(q_out, q_in, q_send, q_recv, peer, me).wait_send()
        tm_copy(k_out, k_in, k_send, k_recv, peer, me).wait_send()
        tm_copy(v_out, v_in, v_send, v_recv, peer, me).wait_send()
        tm_copy(o_out, o_in, o_send, o_recv, peer, me).wait_send()
        return c

    def drain_pack(r, c):
        peer = lax.rem(pk + r, n_pack)
        pack_copy(tags_out, tags_in, tag_send, tag_recv, peer, pk).wait_send()
        pack_copy(pool_out, pool_in, pool_send, pool_recv, peer, pk).wait_send()
        return c

    lax.fori_loop(1, n_tm, drain_tm, 0)
    lax.fori_loop(1, n_pack, drain_pack, 0)
    store.wait()


def local(queries, keys, values, w_out, norm_gain, block_owner, block_base, frame_offset):
    n_tm = lax.axis_size("tm")
    n_pack = lax.axis_size("pack")
    _, frames, width = queries.shape
    lands = n_tm * LANDMARKS
    half = frames // 2
    slot_rows = CAPACITY * WINDOW
    any_ref = pl.BlockSpec(memory_space=pl.ANY)
    vmem = pl.BlockSpec(memory_space=pltpu.VMEM)
    smem = pl.BlockSpec(memory_space=pltpu.SMEM)
    dma = pltpu.SemaphoreType.DMA
    call = pl.pallas_call(
        functools.partial(body, n_tm, n_pack, min(1024, lands)),
        name="landmark_layer",
        out_shape=(
            jax.ShapeDtypeStruct((1, frames, width), BF16),
            jax.ShapeDtypeStruct((1, POOL_DEV, width), BF16),
        ),
        in_specs=[any_ref] * 4 + [vmem, smem, smem, vmem],
        out_specs=(any_ref, vmem),
        scratch_shapes=[
            pltpu.VMEM((frames, width), BF16),
            pltpu.VMEM((frames, width), BF16),
            pltpu.VMEM((frames, width), BF16),
            pltpu.VMEM((width, width), BF16),
            pltpu.VMEM((n_tm, half, LANE), BF16),
            pltpu.VMEM((n_tm, half, LANE), BF16),
            pltpu.VMEM((n_tm, LANDMARKS // 2, LANE), BF16),
            pltpu.VMEM((n_tm, LANDMARKS // 2, LANE), BF16),
            pltpu.VMEM((n_tm, LANDMARKS // 2, LANE), BF16),
            pltpu.VMEM((n_tm, LANDMARKS // 2, LANE), BF16),
            pltpu.VMEM((2, lands, LANE), BF16),
            pltpu.VMEM((2, lands, LANE), BF16),
            pltpu.VMEM((half, lands), F32),
            pltpu.VMEM((half, lands), F32),
            pltpu.VMEM((half, LANE), F32),
            pltpu.VMEM((half, LANE), F32),
            pltpu.VMEM((n_tm, half, LANE), BF16),
            pltpu.VMEM((n_tm, half, LANE), BF16),
            pltpu.VMEM((frames, width), BF16),
            pltpu.VMEM((frames, width), BF16),
            pltpu.VMEM((n_pack * slot_rows, frames), BF16),
            pltpu.VMEM((n_pack, slot_rows, LANE), BF16),
            pltpu.VMEM((n_pack, slot_rows, LANE), BF16),
            pltpu.VMEM((n_pack, slot_rows, width), BF16),
            pltpu.VMEM((n_pack, slot_rows, width), BF16),
            dma((4,)),
            dma((n_tm,)),
            dma((n_tm,)),
            dma((n_tm,)),
            dma((n_tm,)),
            dma((n_tm,)),
            dma((n_tm,)),
            dma((n_tm,)),
            dma((n_tm,)),
            dma((n_pack,)),
            dma((n_pack,)),
            dma((n_pack,)),
            dma((n_pack,)),
            dma(()),
        ],
        compiler_params=pltpu.CompilerParams(
            collective_id=0, has_side_effects=True, vmem_limit_bytes=56 << 20
        ),
        cost_estimate=pl.CostEstimate(
            flops=20_000_000_000, bytes_accessed=8_000_000, transcendentals=36_000_000
        ),
    )
    return call(
        queries,
        keys,
        values,
        w_out,
        norm_gain.reshape(1, width),
        block_owner.reshape(1, -1),
        block_base,
        frame_offset[0],
    )


def solution(mesh):
    return jax.shard_map(
        local,
        mesh=mesh,
        in_specs=(
            P("pack", "tm", None),
            P("pack", "tm", None),
            P("pack", "tm", None),
            P(),
            P(),
            P("pack", "tm", None),
            P("pack", "tm"),
            P("pack", "tm", None),
        ),
        out_specs=(P("pack", "tm", None), P("pack", "tm", None)),
        check_vma=False,
    )
```

```python
import functools

import jax
import jax.numpy as jnp
from jax import lax
from jax.experimental import pallas as pl
from jax.experimental.pallas import tpu as pltpu
from jax.sharding import PartitionSpec as P

HEAD = 64
LANE = 128
LANDMARKS = 256
BLOCK = 128
WINDOW = 16
CAPACITY = 2
POOL_DEV = 128
F32 = jnp.float32
BF16 = jnp.bfloat16
I32 = jnp.int32
MESH = pl.DeviceIdType.MESH
EXP_SCALE = HEAD**-0.5 * 1.4426950408889634


def dot_t(a, b):
    return lax.dot_general(a, b, (((1,), (1,)), ((), ())), preferred_element_type=F32)


def dot(a, b):
    return jnp.dot(a, b, preferred_element_type=F32)


def swap_halves(x):
    return pltpu.roll(x, HEAD, 1)


def body(
    n_tm,
    n_pack,
    chunk,
    q_hbm,
    k_hbm,
    v_hbm,
    w_hbm,
    gain_ref,
    owner_ref,
    base_ref,
    offset_ref,
    enc_hbm,
    pooled_ref,
    q_v,
    k_v,
    v_v,
    w_v,
    q_out,
    q_in,
    k_out,
    k_in,
    v_out,
    v_in,
    k_wide,
    v_wide,
    s_a,
    s_b,
    top_a,
    top_b,
    o_out,
    o_in,
    attended,
    enc_v,
    one_hot,
    tags_out,
    tags_in,
    pool_out,
    pool_in,
    load_sem,
    q_send,
    q_recv,
    k_send,
    k_recv,
    v_send,
    v_recv,
    o_send,
    o_recv,
    tag_send,
    tag_recv,
    pool_send,
    pool_recv,
    store_sem,
):
    me = lax.axis_index("tm")
    pk = lax.axis_index("pack")
    frames, width = q_v.shape
    half_rows = frames // 2
    land_rows = LANDMARKS // 2
    pairs = n_tm // 2
    lands = n_tm * LANDMARKS

    loads = [
        pltpu.make_async_copy(src.at[0] if i < 3 else src, dst, load_sem.at[i])
        for i, (src, dst) in enumerate(((k_hbm, k_v), (q_hbm, q_v), (v_hbm, v_v), (w_hbm, w_v)))
    ]
    for load in loads:
        load.start()

    barrier = pltpu.get_barrier_semaphore()

    def greet_tm(r, c):
        pl.semaphore_signal(
            barrier, inc=1, device_id={"tm": lax.rem(me + r, n_tm)}, device_id_type=MESH
        )
        return c

    def greet_pack(r, c):
        pl.semaphore_signal(
            barrier, inc=1, device_id={"pack": lax.rem(pk + r, n_pack)}, device_id_type=MESH
        )
        return c

    lax.fori_loop(1, n_tm, greet_tm, 0)
    lax.fori_loop(1, n_pack, greet_pack, 0)

    def tm_copy(buffers, peer, source):
        src, dst, send, recv = buffers
        return pltpu.make_async_remote_copy(
            src_ref=src.at[peer],
            dst_ref=dst.at[source],
            send_sem=send.at[peer],
            recv_sem=recv.at[source],
            device_id={"tm": peer},
            device_id_type=MESH,
        )

    def pack_copy(buffers, peer, source):
        src, dst, send, recv = buffers
        return pltpu.make_async_remote_copy(
            src_ref=src.at[peer],
            dst_ref=dst.at[source],
            send_sem=send.at[peer],
            recv_sem=recv.at[source],
            device_id={"pack": peer},
            device_id_type=MESH,
        )

    queries = (q_out, q_in, q_send, q_recv)
    keys = (k_out, k_in, k_send, k_recv)
    values = (v_out, v_in, v_send, v_recv)
    results = (o_out, o_in, o_send, o_recv)
    tags = (tags_out, tags_in, tag_send, tag_recv)
    pools = (pool_out, pool_in, pool_send, pool_recv)

    def target_pair(t):
        return lax.rem(me // 2 + t, pairs)

    def source_pair(t):
        return lax.rem(me // 2 + pairs - t, pairs)

    def send_pair(buffers, pair):
        for member in range(2):
            peer = 2 * pair + member

            @pl.when(peer != me)
            def _():
                tm_copy(buffers, peer, me).start()

    def await_pair(buffers, pair):
        for member in range(2):
            source = 2 * pair + member

            @pl.when(source != me)
            def _():
                tm_copy(buffers, source, source).wait_recv()

    def send_steps(buffers, first, last):
        def one(t, c):
            send_pair(buffers, target_pair(t))
            return c

        lax.fori_loop(first, last, one, 0)

    low = lax.broadcasted_iota(I32, (half_rows, LANE), 1) < HEAD
    low_land = lax.broadcasted_iota(I32, (land_rows, LANE), 1) < HEAD

    def fold(ref, pair, x, mask):
        upper, lower = x[: x.shape[0] // 2], x[x.shape[0] // 2 :]
        ref[2 * pair] = jnp.where(mask, upper, swap_halves(lower)).astype(BF16)
        ref[2 * pair + 1] = jnp.where(mask, swap_halves(upper), lower).astype(BF16)

    def pair_columns(pair):
        return pl.ds(pl.multiple_of(pair * LANE, LANE), LANE)

    average = jnp.where(
        lax.broadcasted_iota(I32, (LANDMARKS, frames), 1) // 2
        == lax.broadcasted_iota(I32, (LANDMARKS, frames), 0),
        0.5,
        0.0,
    ).astype(BF16)

    loads[0].wait()
    per_dot = 2 if pairs % 2 == 0 else 1
    for first in range(0, pairs, per_dot):
        means = dot(average, k_v[:, first * LANE : (first + per_dot) * LANE])
        means = means.astype(BF16).astype(F32)
        for at in range(per_dot):
            fold(k_out, first + at, means[:, at * LANE : (at + 1) * LANE], low_land)
    k_in[me] = k_out[me]
    pl.semaphore_wait(barrier, n_tm + n_pack - 2)
    send_steps(keys, 0, pairs)

    loads[1].wait()
    loads[2].wait()

    def summarize(t):
        pair = target_pair(t)
        cols = pair_columns(pair)
        q, k, v = q_v[:, cols], k_v[:, cols], v_v[:, cols]
        mq = dot(average, q)
        parts = []
        for head in range(2):
            chosen = low if head == 0 else ~low
            s = dot_t(jnp.where(chosen, mq, 0.0).astype(BF16), k)
            p = jnp.exp2((s - jnp.max(s, axis=1, keepdims=True)) * EXP_SCALE)
            total = jnp.sum(p, axis=1, keepdims=True)
            parts.append(dot(p.astype(BF16), v) / total)
        fold(v_out, pair, jnp.where(low, parts[0], parts[1]), low_land)
        fold(q_out, pair, q.astype(F32), low)

    def send_values(t, c):
        summarize(t)
        send_pair(values, target_pair(t))
        return c

    lax.fori_loop(0, pairs, send_values, 0)
    v_in[me] = v_out[me]
    q_in[me] = q_out[me]
    send_steps(queries, 0, pairs)

    slot_rows = CAPACITY * WINDOW
    out_rows = n_pack * slot_rows
    n_blocks = offset_ref.shape[0]
    row_id = lax.broadcasted_iota(I32, (out_rows, LANE), 0)
    owner_id = row_id // slot_rows
    slot_id = (row_id // WINDOW) % CAPACITY
    window_id = row_id % WINDOW
    target = jnp.full((out_rows, LANE), -1, I32)
    tally = jnp.zeros((out_rows, LANE), F32)
    for b in range(n_blocks):
        owner = owner_ref[0, b]
        rank = jnp.int32(0)
        for earlier in range(b):
            rank = rank + jnp.where(owner_ref[0, earlier] == owner, 1, 0)
        mine = (owner_id == owner) & (slot_id == rank)
        target = jnp.where(mine, window_id + base_ref[0, b], target)
        hit = mine & (window_id == offset_ref[b : b + 1, :])
        hit = jnp.where(hit, 1.0, 0.0)
        tally = tally + jnp.sum(hit, axis=1, keepdims=True)
        one_hot[:, b * BLOCK : (b + 1) * BLOCK] = hit.astype(BF16)
    tag_lane = lax.broadcasted_iota(I32, (out_rows, LANE), 1)
    tag = jnp.where(tag_lane == 0, target.astype(F32), tally).astype(BF16)
    for o in range(n_pack):
        tags_out[o] = tag[o * slot_rows : (o + 1) * slot_rows, :]
    tags_in[pk] = tags_out[pk]

    def send_tags(r, c):
        pack_copy(tags, lax.rem(pk + r, n_pack), pk).start()
        return c

    lax.fori_loop(1, n_pack, send_tags, 0)

    def widen(buffers, t, wide, filler):
        pair = source_pair(t)
        await_pair(buffers, pair)
        for member in range(2):
            at = pl.multiple_of((2 * t + member) * LANDMARKS, LANDMARKS)
            upper = pl.ds(at, land_rows)
            lower = pl.ds(at + land_rows, land_rows)
            straight = buffers[1][2 * pair + member].astype(F32)
            swapped = swap_halves(straight)
            wide[0, upper, :] = jnp.where(low_land, straight, filler).astype(BF16)
            wide[0, lower, :] = jnp.where(low_land, swapped, filler).astype(BF16)
            wide[1, upper, :] = jnp.where(low_land, filler, swapped).astype(BF16)
            wide[1, lower, :] = jnp.where(low_land, filler, straight).astype(BF16)

    def widen_keys(t, c):
        widen(keys, t, k_wide, 0.0)
        return c

    def widen_values(t, c):
        widen(values, t, v_wide, 1.0)
        return c

    lax.fori_loop(0, pairs, widen_keys, 0)

    pieces = [slice(at, at + chunk) for at in range(0, lands, chunk)]

    def frames_of(t):
        both = q_in[pl.ds(pl.multiple_of(2 * source_pair(t), 2), 2)]
        return both.reshape(2 * half_rows, LANE)

    def score_piece(q, half, piece, s_ref, top):
        s = dot_t(q, k_wide[half, piece, :])
        s_ref[:, piece] = s
        for at in range(0, chunk, LANE):
            part = s[:, at : at + LANE]
            top = part if top is None else jnp.maximum(top, part)
        return top

    def blend_piece(half, piece, s_ref, top, acc):
        p = jnp.exp2((s_ref[:, piece] - top) * EXP_SCALE).astype(BF16)
        d = dot(p, v_wide[half, piece, :])
        return d if acc is None else acc + d

    def stage(q, half_next, s_next, top_next, half, s_now, top_now):
        top = jnp.max(top_now[...], axis=1, keepdims=True)
        following, acc = None, None
        for piece in pieces:
            if q is not None:
                following = score_piece(q, half_next, piece, s_next, following)
            acc = blend_piece(half, piece, s_now, top, acc)
        if q is not None:
            top_next[...] = following
        return acc

    low_both = lax.broadcasted_iota(I32, (2 * half_rows, LANE), 1) < HEAD

    def finish(t, first, second):
        o = jnp.where(low_both, first / first[:, HEAD : HEAD + 1], second / second[:, 0:1])
        o = o.astype(BF16)
        pair = source_pair(t)
        for member in range(2):
            o_out[2 * pair + member] = o[member * half_rows : (member + 1) * half_rows]
        send_pair(results, pair)

    await_pair(queries, source_pair(0))
    q_start = frames_of(0)
    following = None
    for piece in pieces:
        following = score_piece(q_start, 0, piece, s_a, following)
    top_a[...] = following
    lax.fori_loop(0, pairs, widen_values, 0)

    def attend(t, c):
        await_pair(queries, source_pair(t + 1))
        first = stage(frames_of(t), 1, s_b, top_b, 0, s_a, top_a)
        second = stage(frames_of(t + 1), 0, s_a, top_a, 1, s_b, top_b)
        finish(t, first, second)
        return c

    lax.fori_loop(0, pairs - 1, attend, 0)
    first = stage(frames_of(pairs - 1), 1, s_b, top_b, 0, s_a, top_a)
    second = stage(None, None, None, None, 1, s_b, top_b)
    finish(pairs - 1, first, second)
    o_in[me] = o_out[me]

    def unpack(t, c):
        pair = source_pair(t)
        await_pair(results, pair)
        cols = pair_columns(pair)
        even = o_in[2 * pair].astype(F32)
        odd = o_in[2 * pair + 1].astype(F32)
        attended[0:half_rows, cols] = jnp.where(low, even, swap_halves(odd)).astype(BF16)
        attended[half_rows:frames, cols] = jnp.where(low, swap_halves(even), odd).astype(BF16)
        return c

    lax.fori_loop(0, pairs, unpack, 0)
    loads[3].wait()
    gain = gain_ref[...]

    def project(i, c):
        rows = pl.ds(pl.multiple_of(i * half_rows, half_rows), half_rows)
        projected = dot(attended[rows, :], w_v[...])
        power = jnp.mean(projected * projected, axis=1, keepdims=True)
        enc_v[rows, :] = (projected * lax.rsqrt(power + 1e-6) * gain).astype(BF16)
        return c

    lax.fori_loop(0, 2, project, 0)
    store = pltpu.make_async_copy(enc_v, enc_hbm.at[0], store_sem)
    store.start()

    summed = dot(one_hot[...], enc_v[...]).astype(BF16)
    for o in range(n_pack):
        pool_out[o] = summed[o * slot_rows : (o + 1) * slot_rows, :]
    pool_in[pk] = pool_out[pk]

    def send_pool(r, c):
        pack_copy(pools, lax.rem(pk + r, n_pack), pk).start()
        return c

    lax.fori_loop(1, n_pack, send_pool, 0)

    def drain_tm(r, c):
        peer = lax.rem(me + r, n_tm)
        for buffers in (queries, keys, values, results):
            tm_copy(buffers, peer, me).wait_send()
        return c

    lax.fori_loop(1, n_tm, drain_tm, 0)

    def await_pool(i, c):
        source = lax.rem(pk + i, n_pack)
        pack_copy(tags, source, source).wait_recv()
        pack_copy(pools, source, source).wait_recv()
        return c

    lax.fori_loop(1, n_pack, await_pool, 0)
    tag = tags_in[...].reshape(out_rows, LANE)
    rows = tag.astype(F32)[:, 0:1].astype(I32)
    placing = jnp.where(
        rows == lax.broadcasted_iota(I32, (out_rows, POOL_DEV), 1), 1.0, 0.0
    ).astype(BF16)
    contract = (((0,), (0,)), ((), ()))
    sums = lax.dot_general(
        placing, pool_in[...].reshape(out_rows, width), contract, preferred_element_type=F32
    )
    counts = lax.dot_general(placing, tag, contract, preferred_element_type=F32)[:, 1:2]
    pooled_ref[0] = (sums / jnp.maximum(counts, 1.0)).astype(BF16)

    def drain_pack(r, c):
        for buffers in (tags, pools):
            pack_copy(buffers, lax.rem(pk + r, n_pack), pk).wait_send()
        return c

    lax.fori_loop(1, n_pack, drain_pack, 0)
    store.wait()


def local(queries, keys, values, w_out, norm_gain, block_owner, block_base, frame_offset):
    n_tm = lax.axis_size("tm")
    n_pack = lax.axis_size("pack")
    _, frames, width = queries.shape
    half = frames // 2
    lands = n_tm * LANDMARKS
    slot_rows = CAPACITY * WINDOW
    any_ref = pl.BlockSpec(memory_space=pl.ANY)
    vmem = pl.BlockSpec(memory_space=pltpu.VMEM)
    smem = pl.BlockSpec(memory_space=pltpu.SMEM)
    dma = pltpu.SemaphoreType.DMA
    bf = lambda *shape: pltpu.VMEM(shape, BF16)
    f32 = lambda *shape: pltpu.VMEM(shape, F32)
    return pl.pallas_call(
        functools.partial(body, n_tm, n_pack, min(512, lands)),
        name="landmark_layer",
        out_shape=(
            jax.ShapeDtypeStruct((1, frames, width), BF16),
            jax.ShapeDtypeStruct((1, POOL_DEV, width), BF16),
        ),
        in_specs=[any_ref] * 4 + [vmem, smem, smem, vmem],
        out_specs=(any_ref, vmem),
        scratch_shapes=[
            bf(frames, width),
            bf(frames, width),
            bf(frames, width),
            bf(width, width),
            bf(n_tm, half, LANE),
            bf(n_tm, half, LANE),
            bf(n_tm, LANDMARKS // 2, LANE),
            bf(n_tm, LANDMARKS // 2, LANE),
            bf(n_tm, LANDMARKS // 2, LANE),
            bf(n_tm, LANDMARKS // 2, LANE),
            bf(2, lands, LANE),
            bf(2, lands, LANE),
            f32(frames, lands),
            f32(frames, lands),
            f32(frames, LANE),
            f32(frames, LANE),
            bf(n_tm, half, LANE),
            bf(n_tm, half, LANE),
            bf(frames, width),
            bf(frames, width),
            bf(n_pack * slot_rows, frames),
            bf(n_pack, slot_rows, LANE),
            bf(n_pack, slot_rows, LANE),
            bf(n_pack, slot_rows, width),
            bf(n_pack, slot_rows, width),
            dma((4,)),
        ]
        + [dma((n_tm,))] * 8
        + [dma((n_pack,))] * 4
        + [dma(())],
        compiler_params=pltpu.CompilerParams(
            collective_id=0, has_side_effects=True, vmem_limit_bytes=56 << 20
        ),
        cost_estimate=pl.CostEstimate(
            flops=20_000_000_000, bytes_accessed=8_000_000, transcendentals=36_000_000
        ),
    )(
        queries,
        keys,
        values,
        w_out,
        norm_gain.reshape(1, width),
        block_owner.reshape(1, -1),
        block_base,
        frame_offset[0],
    )


def solution(mesh):
    return jax.shard_map(
        local,
        mesh=mesh,
        in_specs=(
            P("pack", "tm", None),
            P("pack", "tm", None),
            P("pack", "tm", None),
            P(),
            P(),
            P("pack", "tm", None),
            P("pack", "tm"),
            P("pack", "tm", None),
        ),
        out_specs=(P("pack", "tm", None), P("pack", "tm", None)),
        check_vma=False,
    )
```
